256 devices in a mesh: chan: 128 (over y, z, x), tm: 2 (over core).
Axes of the slice: x: 4, y: 4, z: 8, core: 2. Of those that a mesh axis runs over, the one named last changes fastest.
Arguments:
- traces: float32 [16384, 8192], P('chan', 'tm'), may hold values from -600 to 600
- channel_ok: int32 [16384], P('chan'), may hold values 0 or 1
- time_taps: float32 [33], replicated, may hold values from -4 to 4
- space_taps: float32 [5], replicated, may hold values from -4 to 4
- pair_blocks: int32 [2048, 2], P('chan'), may hold values from 0 to 127, as said below
- pair_count: int32 [128], P('chan'), may hold values from 4 to 16, as said below
Outputs:
- stacks: float32 [2048, 201, 128], P(('chan', 'tm'))
The draws below stay inside these ranges and needn't reach their ends.
Inputs may be any that keep to these rules, and one draw needn't show every extreme that they name: `pair_blocks`: a != b, |a - b| <= 4, and both a and b lie within 4 of the owner's index p. Owner p uses its first pair_count[p] slots; the other slots' pairs are ignored. Some owner uses all 16 slots.
All inputs are finite; a program needn't handle non-finite values. No bound on the sum of `channel_ok` on one device may be relied on, other than what follows from the above.
Results may differ from the reference program's by a relative error of at most 0.0049.
Values may be sent and summed in bfloat16 or wider, within the bound.
A program may use at most 128 MiB of HBM per device.

```python
import math
import jax
import jax.numpy as jnp
from jax import lax

BLOCK = 128
SEG = 256
MAXLAG = 100
TAPS = 33
STAPS = 5
CUT = 4
SLOTS = 16
CHANNELS = 16384
SEGMENTS = 32
SAMPLES = 8192
PAIRS = 2048
NFFT = 510
LAGS = 201
N_CHAN = 128


def draw_traces(key, part):
    key_noise, key_chan, key_seg = jax.random.split(key, 3)
    noise = jnp.clip(jax.random.normal(key_noise, (CHANNELS, SAMPLES), jnp.float32), -6.0, 6.0)
    chan_gain = jnp.exp(jax.random.uniform(key_chan, (CHANNELS, 1), jnp.float32, 0.0, 2.3))
    seg_gain = jnp.exp(jax.random.uniform(key_seg, (CHANNELS, SAMPLES // SEG, 1), jnp.float32, 0.0, 2.3))
    seg_gain = jnp.broadcast_to(seg_gain, (CHANNELS, SAMPLES // SEG, SEG)).reshape(CHANNELS, SAMPLES)
    return noise * chan_gain * seg_gain


def draw_pair_blocks(key, part):
    key_first, key_dist = jax.random.split(jax.random.fold_in(key, 11), 2)
    block_count = CHANNELS // BLOCK
    owner_index = jnp.arange(PAIRS, dtype=jnp.int32) // SLOTS
    low_end = jnp.maximum(owner_index - CUT, 0)
    high_end = jnp.minimum(owner_index + CUT, block_count - 1)
    first_block = jax.random.randint(key_first, (PAIRS,), low_end, high_end + 1, jnp.int32)
    distance = jax.random.randint(key_dist, (PAIRS,), 1, CUT + 1, jnp.int32)
    other_end = jnp.where(first_block == high_end, low_end, high_end)
    second_block = jnp.where(first_block + distance <= high_end, first_block + distance, jnp.where(first_block - distance >= low_end, first_block - distance, other_end))
    return jnp.stack([first_block, second_block], axis=1).astype(jnp.int32)


def draw_pair_count(key, part):
    key_level, key_full = jax.random.split(jax.random.fold_in(key, 23), 2)
    block_count = CHANNELS // BLOCK
    level = jax.random.randint(key_level, (block_count,), 0, 3, jnp.int32)
    counts = jnp.where(level == 0, SLOTS, jnp.where(level == 1, SLOTS // 2, SLOTS // 4))
    full_owner = jax.random.randint(key_full, (), 0, block_count, jnp.int32)
    counts = jnp.where(jnp.arange(block_count, dtype=jnp.int32) == full_owner, SLOTS, counts)
    return counts.astype(jnp.int32)


def set_ends(result, rng, least, top_value):
    extent = result.shape
    spot = [jax.random.randint(jax.random.fold_in(rng, axis), (), 0, extent[axis]) for axis in range(len(extent))]
    result = result.at[tuple(spot)].set(least)
    longest = extent.index(max(extent))
    spot[longest] = (spot[longest] + 1) % extent[longest]
    return result.at[tuple(spot)].set(top_value)


def normal_values(rng, dims, scale, limit, kind=jnp.bfloat16):
    entries = jax.random.normal(rng, dims, jnp.float32) * scale
    return jnp.minimum(jnp.maximum(entries, -limit), limit).astype(kind)


def setup_inputs(seed: int = 0) -> dict:
    keys = jax.random.split(jax.random.key(seed), 7)
    return {
        "traces": draw_traces(jax.random.fold_in(keys[6], 71), 0),
        "channel_ok": set_ends((jax.random.randint(keys[1], (CHANNELS,), 0, 8) < 7).astype(jnp.int32), jax.random.fold_in(keys[1], 1), 0, 1),
        "time_taps": normal_values(keys[2], (TAPS,), 1.0, 4.0, jnp.float32),
        "space_taps": normal_values(keys[3], (STAPS,), 1.0, 4.0, jnp.float32),
        "pair_blocks": draw_pair_blocks(jax.random.fold_in(keys[6], 71), 0),
        "pair_count": draw_pair_count(jax.random.fold_in(keys[6], 71), 0),
    }


def dft_matrix():
    sample_pos = jnp.arange(SEG, dtype=jnp.int32)[:, None]
    bin_pos = jnp.arange(SEG, dtype=jnp.int32)[None, :]
    phase_angle = (sample_pos * bin_pos % NFFT).astype(jnp.float32) * (2.0 * math.pi / NFFT)
    return jnp.concatenate([jnp.cos(phase_angle), -jnp.sin(phase_angle)], axis=1).astype(jnp.bfloat16)

def reference(traces, channel_ok, time_taps, space_taps, pair_blocks, pair_count):
    half_taps = (TAPS - 1) // 2
    masked = traces * channel_ok.astype(jnp.float32)[:, None]
    padded = jnp.pad(masked, ((0, 0), (half_taps, half_taps)))
    time_filtered = jnp.zeros_like(masked)
    for tap_index in range(TAPS):
        time_filtered = time_filtered + time_taps[tap_index] * padded[:, tap_index:tap_index + SAMPLES]
    half_space = (STAPS - 1) // 2
    rim_rows = jnp.pad(time_filtered, ((half_space, half_space), (0, 0)))
    filtered = jnp.zeros_like(masked)
    for tap_index in range(STAPS):
        filtered = filtered + space_taps[tap_index] * rim_rows[tap_index:tap_index + CHANNELS]
    segment_view = filtered.reshape(CHANNELS, SEGMENTS, SEG)
    seg_power = lax.optimization_barrier(jnp.mean(segment_view * segment_view, axis=2, keepdims=True))
    whitened = (segment_view / jnp.sqrt(seg_power + 1e-05)).astype(jnp.bfloat16)
    blocks_view = whitened.reshape(N_CHAN, BLOCK, SEGMENTS, SEG)
    dft_table = dft_matrix()

    def transform(block_rows):
        flat_rows = block_rows.reshape(BLOCK * SEGMENTS, SEG)
        spectrum = jnp.dot(flat_rows, dft_table, preferred_element_type=jnp.float32)
        spectrum = spectrum.reshape(BLOCK, SEGMENTS, 2 * SEG)
        return (spectrum[..., :SEG].astype(jnp.bfloat16), spectrum[..., SEG:].astype(jnp.bfloat16))
    spec_real, spec_imag = lax.map(transform, blocks_view)
    count_all = jnp.repeat(pair_count, SLOTS)
    slot_index = jnp.arange(PAIRS, dtype=jnp.int32) % SLOTS
    alive_flag = (slot_index < count_all).astype(jnp.float32)
    lag_index = (jnp.arange(LAGS, dtype=jnp.int32) - MAXLAG) % NFFT
    stack_scale = float(SEGMENTS * SEG) ** (-0.5)

    def correlate(pair_item):
        first_block, second, alive = pair_item
        left_re = spec_real[first_block].astype(jnp.float32)
        left_im = spec_imag[first_block].astype(jnp.float32)
        right_re = spec_real[second].astype(jnp.float32)
        right_im = spec_imag[second].astype(jnp.float32)
        cross_re = lax.optimization_barrier(jnp.sum(left_re * right_re + left_im * right_im, axis=1))
        cross_im = lax.optimization_barrier(jnp.sum(left_im * right_re - left_re * right_im, axis=1))
        lagged = jnp.fft.irfft(lax.complex(cross_re, cross_im), n=NFFT, axis=-1)[:, lag_index]
        return jnp.transpose(lagged) * stack_scale * alive
    return lax.map(correlate, (pair_blocks[:, 0], pair_blocks[:, 1], alive_flag))
```

```python
import functools
import math

import jax
import jax.numpy as jnp
import ml_dtypes
import numpy as np
from jax import lax
from jax.experimental import pallas as pl
from jax.experimental.pallas import tpu as pltpu
from jax.sharding import PartitionSpec as P

SEG = 256
MAXLAG = 100
TAPS = 33
STAPS = 5
CUT = 4
SLOTS = 16
NFFT = 510
LAGS = 201
LAGROWS = 208
BLOCK = 128
GX = 4
CORES = 2
GROUPS = GX * CORES
QG = BLOCK // GROUPS
WIN = 8
PAD = 128
HALF = (TAPS - 1) // 2

BF16 = jnp.bfloat16
F32 = jnp.float32
MESH_ID = pl.DeviceIdType.MESH

OWN_PAIRS = (
    [(i, j) for i in (0, 1) for j in range(2, 6) if j - i <= CUT]
    + [(i, j) for i in range(2, 6) for j in range(i + 1, 6)]
    + [(i, j) for i in (2, 3) for j in (6, 7) if j - i <= CUT]
)
N_DOWN = 7
N_IN = 6
N_UP = 3
N_OWN = len(OWN_PAIRS)
FROM_DN = N_IN + N_UP
FROM_UP = N_DOWN + N_IN
N_ALL = FROM_DN + N_OWN + FROM_UP


def pair_positions():
    table = np.zeros((12 * CUT,), np.int32)
    rel = [(i + 2, j + 2) for i, j in OWN_PAIRS]
    entries = (
        [(i - GX, j - GX) for i, j in rel[N_DOWN:]]
        + rel
        + [(i + GX, j + GX) for i, j in rel[: N_DOWN + N_IN]]
    )
    for spot, (low, high) in enumerate(entries):
        table[low * CUT + high - low - 1] = spot
    return table


def split_np(table):
    high = table.astype(ml_dtypes.bfloat16)
    low = (table - high.astype(np.float64)).astype(ml_dtypes.bfloat16)
    return np.stack([high, low])


def forward_np():
    phase = (np.arange(SEG)[:, None] * np.arange(SEG)[None, :] % NFFT) * (2.0 * np.pi / NFFT)
    return np.concatenate([np.cos(phase), -np.sin(phase)], axis=1).astype(ml_dtypes.bfloat16)


def inverse_np(scale):
    lag = np.arange(LAGS)[None, :] - MAXLAG
    bins = np.arange(SEG)[:, None]
    phase = (lag * bins % NFFT) * (2.0 * np.pi / NFFT)
    weight = np.where((bins == 0) | (bins == SEG - 1), 1.0, 2.0) / NFFT * scale
    table = np.zeros((2 * SEG, SEG), np.float64)
    table[:SEG, :LAGS] = weight * np.cos(phase)
    table[SEG:, :LAGS] = -weight * np.sin(phase)
    return split_np(table)


def order_np():
    table = np.zeros((2, LAGROWS, SEG), ml_dtypes.bfloat16)
    for lag in range(LAGS):
        table[0, lag, lag] = 1.0
        table[1, lag, LAGS - 1 - lag] = 1.0
    return table


def halves(value):
    high = value.astype(BF16)
    return high, (value - high.astype(F32)).astype(BF16)


def dot(a, b):
    return jnp.dot(a, b, preferred_element_type=F32)


def kernel(
    n_chan,
    taps,
    staps,
    pairs,
    count,
    lut,
    ok_row,
    pairs_v,
    fwd,
    inv,
    order,
    traces,
    out,
    xp,
    xh,
    xl,
    band,
    edge,
    rim,
    tfb,
    w,
    r,
    xs,
    c,
    pt,
    f,
    g,
    pbv,
    pbs,
    tr_sem,
    halo_s,
    halo_r,
    pb_s,
    pb_r,
    pb_l,
    x_s,
    x_r,
    z_s,
    z_r,
    p_s,
    p_r,
    f_s,
    f_r,
):
    samples = traces.shape[1]
    n_seg = samples // SEG
    n_chunk = x_s.shape[0]
    per = n_seg // n_chunk
    lines = n_chan // GX
    me = lax.axis_index("chan")
    core = lax.axis_index("tm")
    line = me // GX
    pos = me % GX
    group = pos * CORES + core
    sibling = 1 - core
    nxt = (me + 1) % n_chan
    prv = (me + n_chan - 1) % n_chan
    up = ((line + 1) % lines) * GX + pos
    down = ((line + lines - 1) % lines) * GX + pos
    offsets = [(dx, dt) for dx in range(GX) for dt in range(CORES)]

    def peer(dx, dt):
        return (pos + dx) % GX, (core + dt) % CORES

    load = pltpu.make_async_copy(traces, xp.at[:, pl.ds(PAD, samples)], tr_sem)
    load.start()

    barrier = pltpu.get_barrier_semaphore()
    for dx, dt in offsets[1:]:
        px, pc = peer(dx, dt)
        pl.semaphore_signal(
            barrier, inc=1, device_id=(line * GX + px, pc), device_id_type=MESH_ID
        )
    for other in (up, down, nxt, prv):
        pl.semaphore_signal(barrier, inc=1, device_id=(other, core), device_id_type=MESH_ID)

    band[...] = jnp.zeros_like(band)
    row = lax.broadcasted_iota(jnp.int32, (PAD, PAD), 0)
    col = lax.broadcasted_iota(jnp.int32, (PAD, PAD), 1)
    for diff in range(3):
        index = row - col + (PAD * diff - (PAD - HALF))
        tile = jnp.zeros((PAD, PAD), F32)
        for tap in range(TAPS):
            tile = jnp.where(index == tap, taps[tap], tile)
        high, low = halves(tile)
        for cb in range(2):
            rb = cb + diff
            band[0, rb * PAD : (rb + 1) * PAD, cb * PAD : (cb + 1) * PAD] = high
            band[1, rb * PAD : (rb + 1) * PAD, cb * PAD : (cb + 1) * PAD] = low
    okb = jnp.broadcast_to(ok_row[...], (BLOCK, BLOCK)).astype(F32)
    ok_col = jnp.sum(jnp.where(row == col, okb, 0.0), axis=1, keepdims=True)
    zero_at = pl.multiple_of(core * 0 + jnp.where(core == 0, 0, PAD + samples), PAD)
    xp[:, pl.ds(zero_at, PAD)] = jnp.zeros((BLOCK, PAD), F32)

    load.wait()
    pl.semaphore_wait(barrier, len(offsets) - 1 + 4)

    src_at = pl.multiple_of(jnp.where(core == 0, samples, PAD), PAD)
    dst_at = pl.multiple_of(jnp.where(core == 0, 0, PAD + samples), PAD)
    halo = pltpu.make_async_remote_copy(
        xp.at[:, pl.ds(src_at, PAD)],
        xp.at[:, pl.ds(dst_at, PAD)],
        halo_s.at[0],
        halo_r.at[0],
        device_id=(me, sibling),
        device_id_type=MESH_ID,
    )
    halo.start()

    def pair_copy(dx):
        return pltpu.make_async_remote_copy(
            pairs_v,
            pbv.at[pos],
            pb_s.at[dx - 1],
            pb_r.at[dx - 1],
            device_id=(line * GX + (pos + dx) % GX, core),
            device_id_type=MESH_ID,
        )

    for dx in range(1, GX):
        pair_copy(dx).start()
    pbv[pos] = pairs_v[...]

    halo.wait()

    def mask_step(i, carry):
        at = pl.multiple_of(i * PAD, PAD)
        high, low = halves(xp[:, pl.ds(at, PAD)] * ok_col)
        xh[:, pl.ds(at, PAD)] = high
        xl[:, pl.ds(at, PAD)] = low
        return carry

    lax.fori_loop(0, samples // PAD + 2, mask_step, 0)

    def time_filter(windows_h, windows_l):
        high = jnp.concatenate(windows_h, axis=0)
        low = jnp.concatenate(windows_l, axis=0)
        return dot(high, band[0]) + (dot(low, band[0]) + dot(high, band[1]))

    def edge_step(k, carry):
        wh, wl = [], []
        for i in range(per):
            at = pl.multiple_of((k * per + i) * SEG, SEG)
            for first in (0, BLOCK - 16):
                wh.append(xh[first : first + 16, pl.ds(at, 2 * SEG)])
                wl.append(xl[first : first + 16, pl.ds(at, 2 * SEG)])
        res = time_filter(wh, wl)
        for i in range(per):
            at = pl.multiple_of((k * per + i) * SEG, SEG)
            edge[0, :, pl.ds(at, SEG)] = res[32 * i : 32 * i + 2]
            edge[1, :, pl.ds(at, SEG)] = res[32 * i + 30 : 32 * i + 32]
        return carry

    lax.fori_loop(0, n_chunk, edge_step, 0)
    to_prev = pltpu.make_async_remote_copy(
        edge.at[0], rim.at[1], halo_s.at[1], halo_r.at[1],
        device_id=(prv, core), device_id_type=MESH_ID,
    )
    to_next = pltpu.make_async_remote_copy(
        edge.at[1], rim.at[0], halo_s.at[2], halo_r.at[2],
        device_id=(nxt, core), device_id_type=MESH_ID,
    )
    to_prev.start()
    to_next.start()

    def time_step(k, carry):
        wh, wl = [], []
        for i in range(per):
            at = pl.multiple_of((k * per + i) * SEG, SEG)
            wh.append(xh[:, pl.ds(at, 2 * SEG)])
            wl.append(xl[:, pl.ds(at, 2 * SEG)])
        res = time_filter(wh, wl)
        for i in range(per):
            at = pl.multiple_of((k * per + i) * SEG, SEG)
            tfb[8 : 8 + BLOCK, pl.ds(at, SEG)] = res[i * BLOCK : (i + 1) * BLOCK]
        return carry

    lax.fori_loop(0, n_chunk, time_step, 0)

    to_prev.wait()
    to_next.wait()
    tfb[6:8, :] = jnp.where(me > 0, rim[0], 0.0)
    tfb[8 + BLOCK : 10 + BLOCK, :] = jnp.where(me < n_chan - 1, rim[1], 0.0)

    def chunk_of(k):
        return pl.ds(k * per, per)

    def own_copy(k):
        return pltpu.make_async_copy(
            w.at[group, chunk_of(k)], r.at[2 + pos, core, chunk_of(k)], x_r.at[k, 0]
        )

    def x_copy(k, o):
        px, pc = peer(*offsets[o])
        return pltpu.make_async_remote_copy(
            w.at[px * CORES + pc, chunk_of(k)],
            r.at[2 + pos, core, chunk_of(k)],
            x_s.at[k, o],
            x_r.at[k, o],
            device_id=(line * GX + px, pc),
            device_id_type=MESH_ID,
        )

    def z_copy(k, way):
        if way == 0:
            src, dst, other = r.at[2:4, :, chunk_of(k)], r.at[6:8, :, chunk_of(k)], down
        else:
            src, dst, other = r.at[4:6, :, chunk_of(k)], r.at[0:2, :, chunk_of(k)], up
        return pltpu.make_async_remote_copy(
            src, dst, z_s.at[k, way], z_r.at[k, way],
            device_id=(other, core), device_id_type=MESH_ID,
        )

    def space_step(k, carry):
        for i in range(per):
            at = pl.multiple_of((k * per + i) * SEG, SEG)
            value = staps[0] * tfb[6 : 6 + BLOCK, pl.ds(at, SEG)]
            for tap in range(1, STAPS):
                value = value + staps[tap] * tfb[6 + tap : 6 + tap + BLOCK, pl.ds(at, SEG)]
            power = jnp.sum(value * value, axis=1, keepdims=True) * (1.0 / SEG)
            white = value * (1.0 / jnp.sqrt(power + 1e-05))
            w[:, k * per + i] = white.astype(BF16).reshape(GROUPS, QG, SEG)
        own_copy(k).start()
        for o in (4, 5, 2, 3, 6, 7, 1):
            x_copy(k, o).start()
        return carry

    lax.fori_loop(0, n_chunk, space_step, 0)

    c[...] = jnp.zeros_like(c)

    def receive(k):
        own_copy(k).wait()
        for o in range(1, GROUPS):
            x_copy(k, o).wait_recv()
        z_copy(k, 0).start()
        z_copy(k, 1).start()

    def correlate(k):
        z_copy(k, 0).wait_recv()
        z_copy(k, 1).wait_recv()

        def spectra(h, carry):
            rows = r[pl.ds(4 * h, 4), :, chunk_of(k)].reshape(4 * CORES * per * QG, SEG)
            xs[pl.ds(4 * h, 4)] = dot(rows, fwd[...]).reshape(4, CORES * per, QG, 2 * SEG)
            return carry

        lax.fori_loop(0, 2, spectra, 0)
        for qh in range(QG // 8):
            rows = slice(8 * qh, 8 * qh + 8)
            for kt in range(SEG // 128):
                re_at = slice(128 * kt, 128 * kt + 128)
                im_at = slice(SEG + 128 * kt, SEG + 128 * kt + 128)

                def step(s, acc):
                    re = [xs[b, s, rows, re_at] for b in range(WIN)]
                    im = [xs[b, s, rows, im_at] for b in range(WIN)]
                    new = []
                    for n, (i, j) in enumerate(OWN_PAIRS):
                        new.append(acc[2 * n] + (re[i] * re[j] + im[i] * im[j]))
                        new.append(acc[2 * n + 1] + (im[i] * re[j] - re[i] * im[j]))
                    return tuple(new)

                acc = []
                for n in range(N_OWN):
                    acc.append(c[n, rows, re_at])
                    acc.append(c[n, rows, im_at])
                acc = lax.fori_loop(0, CORES * per, step, tuple(acc))
                for n in range(N_OWN):
                    c[n, rows, re_at] = acc[2 * n]
                    c[n, rows, im_at] = acc[2 * n + 1]

    receive(0)

    def main_step(k, carry):
        receive(k)
        correlate(k - 1)
        return carry

    lax.fori_loop(1, n_chunk, main_step, 0)
    correlate(n_chunk - 1)

    high, low = halves(c[...].reshape(N_OWN * QG, 2 * SEG))
    lagged = dot(high, inv[0]) + (dot(low, inv[0]) + dot(high, inv[1]))
    pt[FROM_DN : FROM_DN + N_OWN] = lagged.astype(BF16).reshape(N_OWN, QG, SEG)
    to_down = pltpu.make_async_remote_copy(
        pt.at[FROM_DN : FROM_DN + FROM_UP],
        pt.at[FROM_DN + N_OWN : N_ALL],
        p_s.at[0], p_r.at[0], device_id=(down, core), device_id_type=MESH_ID,
    )
    to_up = pltpu.make_async_remote_copy(
        pt.at[FROM_DN + N_DOWN : FROM_DN + N_OWN],
        pt.at[0:FROM_DN],
        p_s.at[1], p_r.at[1], device_id=(up, core), device_id_type=MESH_ID,
    )
    to_down.start()
    to_up.start()

    for dx in range(1, GX):
        pair_copy(dx).wait()
    to_smem = pltpu.make_async_copy(pbv, pbs, pb_l)
    to_smem.start()
    to_smem.wait()
    to_down.wait()
    to_up.wait()

    def pick_step(n, carry):
        owner = n // SLOTS
        slot = n % SLOTS
        first = pbs[owner, slot, 0]
        second = pbs[owner, slot, 1]
        lowest = jnp.minimum(first, second) - (line - 1) * GX
        spot = jnp.clip(lowest * CUT + jnp.abs(first - second) - 1, 0, 12 * CUT - 1)
        f[n] = pt[lut[spot]]
        return carry

    lax.fori_loop(0, GX * SLOTS, pick_step, 0)

    half_slots = SLOTS // CORES

    def f_copy(o):
        px, pc = peer(*offsets[o])
        src = f.at[pl.ds(px * SLOTS + pc * half_slots, half_slots)]
        dst = g.at[:, group]
        if o == 0:
            return pltpu.make_async_copy(src, dst, f_r.at[0])
        return pltpu.make_async_remote_copy(
            src, dst, f_s.at[o], f_r.at[o],
            device_id=(line * GX + px, pc), device_id_type=MESH_ID,
        )

    for o in (4, 5, 2, 3, 6, 7, 1, 0):
        f_copy(o).start()
    f_copy(0).wait()
    for o in range(1, GROUPS):
        f_copy(o).wait()

    def out_step(i, carry):
        slot = core * half_slots + i
        back = (pairs[slot, 0] > pairs[slot, 1]).astype(jnp.int32)
        value = lax.dot_general(
            order[back],
            g[i].reshape(BLOCK, SEG),
            (((1,), (1,)), ((), ())),
            preferred_element_type=F32,
        )
        out[i] = jnp.where(slot < count[0], value[:LAGS], 0.0)
        return carry

    lax.fori_loop(0, half_slots, out_step, 0)

    def drain(k, carry):
        for o in range(1, GROUPS):
            x_copy(k, o).wait_send()
        z_copy(k, 0).wait_send()
        z_copy(k, 1).wait_send()
        return carry

    lax.fori_loop(0, n_chunk, drain, 0)


def local(n_chan, traces, channel_ok, time_taps, space_taps, pair_blocks, pair_count):
    samples = traces.shape[1]
    n_seg = samples // SEG
    n_chunk = min(4, n_seg)
    per = n_seg // n_chunk
    scale = 1.0 / math.sqrt(n_seg * CORES * SEG)
    smem = pl.BlockSpec(memory_space=pltpu.SMEM)
    vmem = pl.BlockSpec(memory_space=pltpu.VMEM)
    dma = pltpu.SemaphoreType.DMA
    return pl.pallas_call(
        functools.partial(kernel, n_chan),
        out_shape=jax.ShapeDtypeStruct((SLOTS // CORES, LAGS, BLOCK), F32),
        in_specs=[smem, smem, smem, smem, smem, vmem, vmem, vmem, vmem, vmem,
                  pl.BlockSpec(memory_space=pl.ANY)],
        out_specs=vmem,
        scratch_shapes=[
            pltpu.VMEM((BLOCK, samples + 2 * PAD), F32),
            pltpu.VMEM((BLOCK, samples + 2 * PAD), BF16),
            pltpu.VMEM((BLOCK, samples + 2 * PAD), BF16),
            pltpu.VMEM((2, 2 * SEG, SEG), BF16),
            pltpu.VMEM((2, 2, samples), F32),
            pltpu.VMEM((2, 2, samples), F32),
            pltpu.VMEM((BLOCK + 16, samples), F32),
            pltpu.VMEM((GROUPS, n_seg, QG, SEG), BF16),
            pltpu.VMEM((WIN, CORES, n_seg, QG, SEG), BF16),
            pltpu.VMEM((WIN, CORES * per, QG, 2 * SEG), F32),
            pltpu.VMEM((N_OWN, QG, 2 * SEG), F32),
            pltpu.VMEM((N_ALL, QG, SEG), BF16),
            pltpu.VMEM((GX * SLOTS, QG, SEG), BF16),
            pltpu.VMEM((SLOTS // CORES, GROUPS, QG, SEG), BF16),
            pltpu.VMEM((GX, SLOTS, 2), jnp.int32),
            pltpu.SMEM((GX, SLOTS, 2), jnp.int32),
            dma,
            dma((3,)),
            dma((3,)),
            dma((3,)),
            dma((3,)),
            dma,
            dma((n_chunk, GROUPS)),
            dma((n_chunk, GROUPS)),
            dma((n_chunk, 2)),
            dma((n_chunk, 2)),
            dma((2,)),
            dma((2,)),
            dma((GROUPS,)),
            dma((GROUPS,)),
        ],
        compiler_params=pltpu.CompilerParams(
            collective_id=0, has_side_effects=True, vmem_limit_bytes=48 * 1024 * 1024
        ),
    )(
        time_taps,
        space_taps,
        pair_blocks,
        pair_count,
        jnp.asarray(pair_positions()),
        channel_ok.reshape(1, BLOCK),
        pair_blocks,
        jnp.asarray(forward_np()),
        jnp.asarray(inverse_np(scale)),
        jnp.asarray(order_np()),
        traces,
    )


def solution(mesh):
    return jax.shard_map(
        functools.partial(local, mesh.shape["chan"]),
        mesh=mesh,
        in_specs=(P("chan", "tm"), P("chan"), P(), P(), P("chan", None), P("chan")),
        out_specs=P(("chan", "tm"), None, None),
        check_vma=False,
    )
```

```python
import functools
import math

import jax
import jax.numpy as jnp
import ml_dtypes
import numpy as np
from jax import lax
from jax.experimental import pallas as pl
from jax.experimental.pallas import tpu as pltpu
from jax.sharding import PartitionSpec as P

SEG = 256
MAXLAG = 100
TAPS = 33
STAPS = 5
CUT = 4
SLOTS = 16
NFFT = 510
LAGS = 201
LAGROWS = 208
BLOCK = 128
GX = 4
CORES = 2
GROUPS = GX * CORES
QG = BLOCK // GROUPS
WIN = 8
PAD = 128
HALF = (TAPS - 1) // 2
CHUNKS = 8

BF16 = jnp.bfloat16
F32 = jnp.float32
MESH_ID = pl.DeviceIdType.MESH

OWN_PAIRS = (
    [(i, j) for i in (0, 1) for j in range(2, 6) if j - i <= CUT]
    + [(i, j) for i in range(2, 6) for j in range(i + 1, 6)]
    + [(i, j) for i in (2, 3) for j in (6, 7) if j - i <= CUT]
)
N_DOWN = 7
N_IN = 6
N_UP = 3
N_OWN = len(OWN_PAIRS)
FROM_DN = N_IN + N_UP
FROM_UP = N_DOWN + N_IN
N_ALL = FROM_DN + N_OWN + FROM_UP


def pair_positions():
    table = np.zeros((12 * CUT,), np.int32)
    rel = [(i + 2, j + 2) for i, j in OWN_PAIRS]
    entries = (
        [(i - GX, j - GX) for i, j in rel[N_DOWN:]]
        + rel
        + [(i + GX, j + GX) for i, j in rel[: N_DOWN + N_IN]]
    )
    for spot, (low, high) in enumerate(entries):
        table[low * CUT + high - low - 1] = spot
    return table


def split_np(table):
    high = table.astype(ml_dtypes.bfloat16)
    low = (table - high.astype(np.float64)).astype(ml_dtypes.bfloat16)
    return np.stack([high, low])


def forward_np():
    phase = (np.arange(SEG)[:, None] * np.arange(SEG)[None, :] % NFFT) * (2.0 * np.pi / NFFT)
    return np.concatenate([np.cos(phase), -np.sin(phase)], axis=1).astype(ml_dtypes.bfloat16)


def inverse_np(scale):
    lag = np.arange(LAGS)[None, :] - MAXLAG
    bins = np.arange(SEG)[:, None]
    phase = (lag * bins % NFFT) * (2.0 * np.pi / NFFT)
    weight = np.where((bins == 0) | (bins == SEG - 1), 1.0, 2.0) / NFFT * scale
    table = np.zeros((2 * SEG, SEG), np.float64)
    table[:SEG, :LAGS] = weight * np.cos(phase)
    table[SEG:, :LAGS] = -weight * np.sin(phase)
    return split_np(table)


def order_np():
    table = np.zeros((2, LAGROWS, SEG), ml_dtypes.bfloat16)
    for lag in range(LAGS):
        table[0, lag, lag] = 1.0
        table[1, lag, LAGS - 1 - lag] = 1.0
    return table


def halves(value):
    high = value.astype(BF16)
    return high, (value - high.astype(F32)).astype(BF16)


def dot(a, b):
    return jnp.dot(a, b, preferred_element_type=F32)


def kernel(
    n_chan,
    taps_h,
    staps_h,
    pairs_h,
    count_h,
    lut_h,
    ok_h,
    fwd_h,
    inv_h,
    order_h,
    traces,
    out,
    taps,
    staps,
    pairs,
    count,
    lut,
    ok_row,
    fwd,
    inv,
    order,
    okn,
    xp,
    hx,
    xh,
    xl,
    hxh,
    hxl,
    band,
    tfb,
    w,
    r,
    xs,
    c,
    pt0,
    pt1,
    f,
    g,
    pbv,
    pbs,
    spots,
    in_sem,
    own_sem,
    halo_s,
    halo_r,
    pb_s,
    pb_r,
    pb_l,
    x_s,
    x_r,
    z_s,
    z_r,
    p_s,
    p_r,
    f_s,
    f_r,
):
    samples = traces.shape[1]
    n_seg = samples // SEG
    n_chunk = x_s.shape[0]
    per = n_seg // n_chunk
    lines = n_chan // GX
    me = lax.axis_index("chan")
    core = lax.axis_index("tm")
    line = me // GX
    pos = me % GX
    group = pos * CORES + core
    sibling = 1 - core
    nxt = (me + 1) % n_chan
    prv = (me + n_chan - 1) % n_chan
    up = ((line + 1) % lines) * GX + pos
    down = ((line + lines - 1) % lines) * GX + pos
    offsets = [(dx, dt) for dx in range(GX) for dt in range(CORES)]
    half_slots = SLOTS // CORES

    def peer(dx, dt):
        return (pos + dx) % GX, (core + dt) % CORES

    def remote(src, dst, send, recv, chan, tm):
        return pltpu.make_async_remote_copy(
            src, dst, send, recv, device_id=(chan, tm), device_id_type=MESH_ID
        )

    barrier = pltpu.get_barrier_semaphore()
    for dx, dt in offsets[1:]:
        px, pc = peer(dx, dt)
        pl.semaphore_signal(
            barrier, inc=1, device_id=(line * GX + px, pc), device_id_type=MESH_ID
        )
    for other in (up, down, nxt, prv):
        pl.semaphore_signal(barrier, inc=1, device_id=(other, core), device_id_type=MESH_ID)

    loads = [
        pltpu.make_async_copy(src, dst, in_sem.at[n])
        for n, (src, dst) in enumerate(
            [
                (taps_h, taps),
                (ok_h, ok_row),
                (traces, xp.at[:, pl.ds(PAD, samples)]),
                (staps_h, staps),
                (fwd_h, fwd),
                (pairs_h, pairs),
                (count_h, count),
                (lut_h, lut),
                (inv_h, inv),
                (order_h, order),
            ]
        )
    ]
    for load in loads:
        load.start()

    def at_of(j):
        return pl.multiple_of(jnp.where(core == 0, j, n_seg - 1 - j) * SEG, SEG)

    zero_at = pl.multiple_of(jnp.where(core == 0, 0, PAD + samples), PAD)
    pad_at = pl.multiple_of(jnp.where(core == 0, PAD + samples, 0), PAD)
    src_at = pl.multiple_of(jnp.where(core == 0, samples, PAD), PAD)
    xp[:, pl.ds(zero_at, PAD)] = jnp.zeros((BLOCK, PAD), F32)
    hx[:, pl.ds(zero_at, PAD)] = jnp.zeros((16, PAD), F32)

    loads[0].wait()
    band[...] = jnp.zeros_like(band)
    row = lax.broadcasted_iota(jnp.int32, (PAD, PAD), 0)
    col = lax.broadcasted_iota(jnp.int32, (PAD, PAD), 1)
    for diff in range(3):
        index = row - col + (PAD * diff - (PAD - HALF))
        tile = jnp.zeros((PAD, PAD), F32)
        for tap in range(TAPS):
            tile = jnp.where(index == tap, taps[tap], tile)
        high, low = halves(tile)
        for cb in range(2):
            rb = cb + diff
            band[0, rb * PAD : (rb + 1) * PAD, cb * PAD : (cb + 1) * PAD] = high
            band[1, rb * PAD : (rb + 1) * PAD, cb * PAD : (cb + 1) * PAD] = low
    loads[1].wait()
    okb = jnp.broadcast_to(ok_row[...], (BLOCK, BLOCK)).astype(F32)
    ok_col = jnp.sum(jnp.where(row == col, okb, 0.0), axis=1, keepdims=True)

    loads[2].wait()
    pl.semaphore_wait(barrier, len(offsets) - 1 + 4)

    to_next = remote(
        traces.at[BLOCK - 2 : BLOCK], hx.at[6:8, pl.ds(PAD, samples)],
        halo_s.at[1], halo_r.at[1], nxt, core,
    )
    to_prev = remote(
        traces.at[0:2], hx.at[8:10, pl.ds(PAD, samples)],
        halo_s.at[2], halo_r.at[2], prv, core,
    )
    ok_next = remote(ok_h, okn.at[0], halo_s.at[3], halo_r.at[3], nxt, core)
    ok_prev = remote(ok_h, okn.at[1], halo_s.at[4], halo_r.at[4], prv, core)
    halo = remote(
        xp.at[:, pl.ds(src_at, PAD)], xp.at[:, pl.ds(zero_at, PAD)],
        halo_s.at[0], halo_r.at[0], me, sibling,
    )
    corner_next = remote(
        xp.at[BLOCK - 2 : BLOCK, pl.ds(pad_at, PAD)], hx.at[6:8, pl.ds(pad_at, PAD)],
        halo_s.at[5], halo_r.at[5], nxt, core,
    )
    corner_prev = remote(
        xp.at[0:2, pl.ds(pad_at, PAD)], hx.at[8:10, pl.ds(pad_at, PAD)],
        halo_s.at[6], halo_r.at[6], prv, core,
    )

    def pair_copy(dx):
        return remote(
            pairs_h, pbv.at[pos], pb_s.at[dx - 1], pb_r.at[dx - 1],
            line * GX + (pos + dx) % GX, core,
        )

    own_pairs = pltpu.make_async_copy(pairs_h, pbv.at[pos], pb_l.at[0])
    to_smem = pltpu.make_async_copy(pbv, pbs, pb_l.at[1])

    for copy in (to_next, to_prev, ok_next, ok_prev, halo):
        copy.start()
    for dx in range(1, GX):
        pair_copy(dx).start()
    own_pairs.start()

    def mask_at(at):
        high, low = halves(xp[:, pl.ds(at, PAD)] * ok_col)
        xh[:, pl.ds(at, PAD)] = high
        xl[:, pl.ds(at, PAD)] = low

    def mask_step(i, carry):
        mask_at(pl.multiple_of((i + 1) * PAD, PAD))
        return carry

    lax.fori_loop(0, samples // PAD, mask_step, 0)
    mask_at(zero_at)

    def time_filter(windows_h, windows_l):
        high = jnp.concatenate(windows_h, axis=0)
        low = jnp.concatenate(windows_l, axis=0)
        return dot(high, band[0]) + (dot(low, band[0]) + dot(high, band[1]))

    def time_step(k):
        spot = [at_of(k * per + i) for i in range(per)]
        res = time_filter(
            [xh[:, pl.ds(at, 2 * SEG)] for at in spot],
            [xl[:, pl.ds(at, 2 * SEG)] for at in spot],
        )
        for i, at in enumerate(spot):
            tfb[8 : 8 + BLOCK, pl.ds(at, SEG)] = res[i * BLOCK : (i + 1) * BLOCK]

    def rim_step(steps):
        spot = [at_of(j) for j in steps]
        res = time_filter(
            [hxh[:, pl.ds(at, 2 * SEG)] for at in spot],
            [hxl[:, pl.ds(at, 2 * SEG)] for at in spot],
        )
        for i, at in enumerate(spot):
            tfb[0:8, pl.ds(at, SEG)] = res[16 * i : 16 * i + 8]
            tfb[8 + BLOCK : 16 + BLOCK, pl.ds(at, SEG)] = res[16 * i + 8 : 16 * i + 16]

    time_step(0)

    halo.wait()
    corner_next.start()
    corner_prev.start()
    mask_at(pad_at)

    for copy in (to_next, to_prev, ok_next, ok_prev):
        copy.wait()
    rim_row = lax.broadcasted_iota(jnp.int32, (16, BLOCK), 0)
    rim_col = lax.broadcasted_iota(jnp.int32, (16, BLOCK), 1)
    is_top = (rim_row >= 6) & (rim_row < 8) & (rim_col == rim_row + (BLOCK - 8)) & (me > 0)
    is_low = (rim_row >= 8) & (rim_row < 10) & (rim_col == rim_row - 8) & (me < n_chan - 1)
    ok_top = jnp.broadcast_to(okn[0], (16, BLOCK)).astype(F32)
    ok_low = jnp.broadcast_to(okn[1], (16, BLOCK)).astype(F32)
    ok_rim = jnp.sum(
        jnp.where(is_top, ok_top, jnp.where(is_low, ok_low, 0.0)), axis=1, keepdims=True
    )

    def rim_mask(at, width):
        rows = lax.broadcasted_iota(jnp.int32, (16, width), 0)
        high, low = halves(
            jnp.where((rows >= 6) & (rows < 10), hx[:, pl.ds(at, width)], 0.0) * ok_rim
        )
        hxh[:, pl.ds(at, width)] = high
        hxl[:, pl.ds(at, width)] = low

    def rim_mask_step(i, carry):
        rim_mask(pl.multiple_of(PAD + i * 2 * SEG, PAD), 2 * SEG)
        return carry

    lax.fori_loop(0, samples // (2 * SEG), rim_mask_step, 0)
    rim_mask(zero_at, PAD)
    rim_step(range(n_seg - 1))

    def chunk_of(k):
        return pl.ds(k * per, per)

    def own_copy(k):
        return pltpu.make_async_copy(
            w.at[group, chunk_of(k)], r.at[2 + pos, core, chunk_of(k)], own_sem.at[k]
        )

    def x_copy(k, o):
        px, pc = peer(*offsets[o])
        return remote(
            w.at[px * CORES + pc, chunk_of(k)], r.at[2 + pos, core, chunk_of(k)],
            x_s.at[k, o], x_r.at[k, o], line * GX + px, pc,
        )

    def z_copy(k, way):
        if way == 0:
            src, dst, other = r.at[2:4, :, chunk_of(k)], r.at[6:8, :, chunk_of(k)], down
        else:
            src, dst, other = r.at[4:6, :, chunk_of(k)], r.at[0:2, :, chunk_of(k)], up
        return remote(src, dst, z_s.at[k, way], z_r.at[k, way], other, core)

    def space_step(k):
        for i in range(per):
            at = at_of(k * per + i)
            value = staps[0] * tfb[6 : 6 + BLOCK, pl.ds(at, SEG)]
            for tap in range(1, STAPS):
                value = value + staps[tap] * tfb[6 + tap : 6 + tap + BLOCK, pl.ds(at, SEG)]
            power = jnp.sum(value * value, axis=1, keepdims=True) * (1.0 / SEG)
            white = value * (1.0 / jnp.sqrt(power + 1e-05))
            w[:, k * per + i] = white.astype(BF16).reshape(GROUPS, QG, SEG)
        for o in (4, 5, 2, 3, 6, 7, 1):
            x_copy(k, o).start()
        own_copy(k).start()

    def receive(k):
        own_copy(k).wait()
        for o in range(1, GROUPS):
            x_copy(k, o).wait_recv()
        z_copy(k, 0).start()
        z_copy(k, 1).start()

    def correlate(k):
        z_copy(k, 0).wait_recv()
        z_copy(k, 1).wait_recv()

        def spectra(h, carry):
            rows = r[pl.ds(4 * h, 4), :, chunk_of(k)].reshape(4 * CORES * per * QG, SEG)
            xs[pl.ds(4 * h, 4)] = dot(rows, fwd[...]).reshape(4, CORES * per, QG, 2 * SEG)
            return carry

        lax.fori_loop(0, 2, spectra, 0)
        for qh in range(QG // 8):
            rows = slice(8 * qh, 8 * qh + 8)
            for kt in range(SEG // 128):
                re_at = slice(128 * kt, 128 * kt + 128)
                im_at = slice(SEG + 128 * kt, SEG + 128 * kt + 128)

                def step(s, acc):
                    re = [xs[b, s, rows, re_at] for b in range(WIN)]
                    im = [xs[b, s, rows, im_at] for b in range(WIN)]
                    new = []
                    for n, (i, j) in enumerate(OWN_PAIRS):
                        new.append(acc[2 * n] + (re[i] * re[j] + im[i] * im[j]))
                        new.append(acc[2 * n + 1] + (im[i] * re[j] - re[i] * im[j]))
                    return tuple(new)

                acc = []
                for n in range(N_OWN):
                    acc.append(c[n, rows, re_at])
                    acc.append(c[n, rows, im_at])
                acc = lax.fori_loop(0, CORES * per, step, tuple(acc))
                for n in range(N_OWN):
                    c[n, rows, re_at] = acc[2 * n]
                    c[n, rows, im_at] = acc[2 * n + 1]

    def find_spots():
        for dx in range(1, GX):
            pair_copy(dx).wait()
        own_pairs.wait()
        for load in loads[3:]:
            if load is not loads[3] and load is not loads[4]:
                load.wait()
        to_smem.start()
        to_smem.wait()

        def spot_step(n, carry):
            owner = n // SLOTS
            slot = n % SLOTS
            first = pbs[owner, 0, slot]
            second = pbs[owner, 1, slot]
            lowest = jnp.minimum(first, second) - (line - 1) * GX
            index = jnp.clip(lowest * CUT + jnp.abs(first - second) - 1, 0, 12 * CUT - 1)
            spots[n] = lut[index]
            return carry

        lax.fori_loop(0, GX * SLOTS, spot_step, 0)

    c[...] = jnp.zeros_like(c)
    loads[3].wait()
    loads[4].wait()

    def tick(i, carry):
        @pl.when(i < n_chunk)
        def _():
            space_step(i)

        @pl.when((i >= 2) & (i < n_chunk + 2))
        def _():
            receive(i - 2)

        @pl.when(i + 1 < n_chunk)
        def _():
            time_step(i + 1)

        @pl.when(i == n_chunk - 2)
        def _():
            corner_next.wait()
            corner_prev.wait()
            rim_mask(pad_at, PAD)
            rim_step([n_seg - 1])

        @pl.when(i == 3)
        def _():
            find_spots()

        @pl.when(i >= 4)
        def _():
            correlate(i - 4)

        return carry

    lax.fori_loop(0, n_chunk + 4, tick, 0)

    pt = (pt0, pt1)

    def to_down(h):
        return remote(
            pt[h].at[FROM_DN : FROM_DN + FROM_UP], pt[h].at[FROM_DN + N_OWN : N_ALL],
            p_s.at[h, 0], p_r.at[h, 0], down, core,
        )

    def to_up(h):
        return remote(
            pt[h].at[FROM_DN + N_DOWN : FROM_DN + N_OWN], pt[h].at[0:FROM_DN],
            p_s.at[h, 1], p_r.at[h, 1], up, core,
        )

    for h in range(2):
        high, low = halves(c[:, 8 * h : 8 * h + 8].reshape(N_OWN * 8, 2 * SEG))
        lagged = dot(high, inv[0]) + (dot(low, inv[0]) + dot(high, inv[1]))
        pt[h][FROM_DN : FROM_DN + N_OWN] = lagged.astype(BF16).reshape(N_OWN, 8, SEG)
        to_down(h).start()
        to_up(h).start()

    def f_copy(h, o):
        px, pc = peer(*offsets[o])
        src = f.at[h, pl.ds(px * SLOTS + pc * half_slots, half_slots)]
        dst = g.at[:, group, h]
        if o == 0:
            return pltpu.make_async_copy(src, dst, f_r.at[h, 0])
        return remote(src, dst, f_s.at[h, o], f_r.at[h, o], line * GX + px, pc)

    for h in range(2):
        to_down(h).wait()
        to_up(h).wait()

        def pick_step(n, carry):
            for i in range(8):
                f[h, n * 8 + i] = pt[h][spots[n * 8 + i]]
            return carry

        lax.fori_loop(0, GX * SLOTS // 8, pick_step, 0)
        for o in (4, 5, 2, 3, 6, 7, 1, 0):
            f_copy(h, o).start()

    def drain(k, carry):
        for o in range(1, GROUPS):
            x_copy(k, o).wait_send()
        z_copy(k, 0).wait_send()
        z_copy(k, 1).wait_send()
        return carry

    lax.fori_loop(0, n_chunk, drain, 0)
    for h in range(2):
        for o in range(GROUPS):
            f_copy(h, o).wait()

    for i in range(half_slots):
        slot = core * half_slots + i
        back = (pairs[0, slot] > pairs[1, slot]).astype(jnp.int32)
        value = lax.dot_general(
            order[back],
            g[i].reshape(BLOCK, SEG),
            (((1,), (1,)), ((), ())),
            preferred_element_type=F32,
        )
        out[:, i, :] = jnp.where(slot < count[0], value[:LAGS], 0.0)


def local(n_chan, traces, channel_ok, time_taps, space_taps, pair_blocks, pair_count):
    samples = traces.shape[1]
    n_seg = samples // SEG
    n_chunk = CHUNKS
    per = n_seg // n_chunk
    scale = 1.0 / math.sqrt(n_seg * CORES * SEG)
    hbm = pl.BlockSpec(memory_space=pltpu.HBM)
    dma = pltpu.SemaphoreType.DMA
    wide = samples + 2 * PAD
    half_slots = SLOTS // CORES
    res = pl.pallas_call(
        functools.partial(kernel, n_chan),
        out_shape=jax.ShapeDtypeStruct((LAGS, half_slots, BLOCK), F32),
        in_specs=[hbm] * 10,
        out_specs=pl.BlockSpec(memory_space=pltpu.VMEM),
        scratch_shapes=[
            pltpu.SMEM((TAPS,), F32),
            pltpu.SMEM((STAPS,), F32),
            pltpu.SMEM((2, SLOTS), jnp.int32),
            pltpu.SMEM((1,), jnp.int32),
            pltpu.SMEM((12 * CUT,), jnp.int32),
            pltpu.VMEM((1, BLOCK), jnp.int32),
            pltpu.VMEM((SEG, 2 * SEG), BF16),
            pltpu.VMEM((2, 2 * SEG, SEG), BF16),
            pltpu.VMEM((2, LAGROWS, SEG), BF16),
            pltpu.VMEM((2, 1, BLOCK), jnp.int32),
            pltpu.VMEM((BLOCK, wide), F32),
            pltpu.VMEM((16, wide), F32),
            pltpu.VMEM((BLOCK, wide), BF16),
            pltpu.VMEM((BLOCK, wide), BF16),
            pltpu.VMEM((16, wide), BF16),
            pltpu.VMEM((16, wide), BF16),
            pltpu.VMEM((2, 2 * SEG, SEG), BF16),
            pltpu.VMEM((BLOCK + 16, samples), F32),
            pltpu.VMEM((GROUPS, n_seg, QG, SEG), BF16),
            pltpu.VMEM((WIN, CORES, n_seg, QG, SEG), BF16),
            pltpu.VMEM((WIN, CORES * per, QG, 2 * SEG), F32),
            pltpu.VMEM((N_OWN, QG, 2 * SEG), F32),
            pltpu.VMEM((N_ALL, 8, SEG), BF16),
            pltpu.VMEM((N_ALL, 8, SEG), BF16),
            pltpu.VMEM((2, GX * SLOTS, 8, SEG), BF16),
            pltpu.VMEM((half_slots, GROUPS, 2, 8, SEG), BF16),
            pltpu.VMEM((GX, 2, SLOTS), jnp.int32),
            pltpu.SMEM((GX, 2, SLOTS), jnp.int32),
            pltpu.SMEM((GX * SLOTS,), jnp.int32),
            dma((10,)),
            dma((n_chunk,)),
            dma((7,)),
            dma((7,)),
            dma((3,)),
            dma((3,)),
            dma((2,)),
            dma((n_chunk, GROUPS)),
            dma((n_chunk, GROUPS)),
            dma((n_chunk, 2)),
            dma((n_chunk, 2)),
            dma((2, 2)),
            dma((2, 2)),
            dma((2, GROUPS)),
            dma((2, GROUPS)),
        ],
        compiler_params=pltpu.CompilerParams(
            collective_id=0, has_side_effects=True, vmem_limit_bytes=67043328
        ),
    )(
        time_taps,
        space_taps,
        jnp.transpose(pair_blocks),
        pair_count,
        jnp.asarray(pair_positions()),
        channel_ok.reshape(1, BLOCK),
        jnp.asarray(forward_np()),
        jnp.asarray(inverse_np(scale)),
        jnp.asarray(order_np()),
        traces,
    )
    return jnp.transpose(res, (1, 0, 2))


def solution(mesh):
    return jax.shard_map(
        functools.partial(local, mesh.shape["chan"]),
        mesh=mesh,
        in_specs=(P("chan", "tm"), P("chan"), P(), P(), P("chan", None), P("chan")),
        out_specs=P(("chan", "tm"), None, None),
        check_vma=False,
    )
```
